32 devices in a mesh: section: 2 (over core), experts: 4 (over z), dp: 4 (over y, x).
Axes of the slice: x: 2, y: 2, z: 4, core: 2. Of those that a mesh axis runs over, the one named last changes fastest.
Arguments:
- tokens: bfloat16 [6304, 768], P(('experts', 'dp')), may hold values from -6 to 6
- cotangent: bfloat16 [6304, 768], P(('experts', 'dp')), may hold values from -6 to 6
- norm_gains: float32 [2, 2, 768], P('section'), may hold values from 0.5 to 1.5
- norm_biases: float32 [2, 2, 768], P('section'), may hold values from -1.5 to 1.5
- qkv_weight: bfloat16 [2, 768, 2304], P('section'), may hold values from -4 to 4
- out_weight: bfloat16 [2, 768, 768], P('section'), may hold values from -1.5 to 1.5
- dense_in: bfloat16 [768, 3072], replicated, may hold values from -0.21875 to 0.21875
- dense_out: bfloat16 [3072, 768], replicated, may hold values from -0.109375 to 0.109375
- expert_in: bfloat16 [4, 768, 3072], P('experts', None, 'dp'), may hold values from -0.21875 to 0.21875
- expert_out: bfloat16 [4, 3072, 768], P('experts', 'dp'), may hold values from -0.109375 to 0.109375
- routes: int32 [6304, 2], P(('experts', 'dp')), may hold values from 0 to 3, all different within a row
- gates: float32 [6304, 2], P(('experts', 'dp')), may hold values from 0.1 to 0.6
Outputs:
- acts: bfloat16 [2, 6304, 768], P('section', ('experts', 'dp'))
- act_grads: float32 [2, 6304, 768], P('section', ('experts', 'dp'))
- qkv_grad: float32 [2, 768, 2304], P('section', ('experts', 'dp'))
- out_grad: float32 [2, 768, 768], P('section', ('experts', 'dp'))
- gain_grad: float32 [2, 2, 768], P('section', None, ('experts', 'dp'))
- bias_grad: float32 [2, 2, 768], P('section', None, ('experts', 'dp'))
- dense_in_grad: float32 [768, 3072], P(('experts', 'dp'), 'section')
- dense_out_grad: float32 [3072, 768], P(('experts', 'dp'), 'section')
- expert_in_grad: float32 [4, 768, 3072], P('experts', 'section', 'dp')
- expert_out_grad: float32 [4, 3072, 768], P('experts', 'dp', 'section')
The draws below stay inside these ranges and needn't reach their ends.
Inputs may be any that keep to these rules, and one draw needn't show every extreme that they name: `routes`: each row names two different experts, and every expert is named by some row.
All inputs are finite; a program needn't handle non-finite values.
Results may differ from the reference program's by a relative error of at most 0.015.
The reference program's roundings to bfloat16 on the way count: a program that leaves them out, or rounds other values in their place, can miss the bound.
Values may be sent and summed in bfloat16 or wider, within the bound.
A program may use at most 448 MiB of HBM per device.

```python
import math
import jax
import jax.numpy as jnp
from jax import lax

D = 768
HEADS = 12
HEAD_DIM = 64
FF = 3072
SEQ = 197
ROWS = 197
TOKENS = 6304
EXPERTS = 4
CAP = 98


def draw_qkv_weight(key, part):
    base_key = jax.random.fold_in(jax.random.fold_in(key, 17), 0)
    weights = jax.random.normal(base_key, (2, D, 3 * D), jnp.float32) / math.sqrt(D)
    return jnp.clip(weights, -4.0, 4.0).astype(jnp.bfloat16)


def shard_levels(key, extent, shards, smallest, high):
    level, own = 1.0, jax.random.fold_in(key, 6)
    for axis_at, blocks in shards:
        heights = jnp.exp(jax.random.uniform(jax.random.fold_in(own, axis_at), (blocks,), jnp.float32, smallest / len(shards), high / len(shards)))
        level = level * jnp.repeat(heights, extent[axis_at] // blocks).reshape([-1 if axis == axis_at else 1 for axis in range(len(extent))])
    return level


def distinct(key, rows, amount, top, lift):
    ranking = jax.random.permutation(jax.random.fold_in(key, 1), amount)
    boost = ranking
    for power in range(3):
        boost = boost * boost // amount
    boost = boost * lift // amount
    tickets = jax.random.randint(jax.random.fold_in(key, 2), (rows, amount), 0, 4096) + boost
    sure = jax.random.permutation(jax.random.fold_in(key, 3), rows)[jnp.arange(amount) % rows]
    tickets = jnp.where(jnp.arange(rows)[:, None] == sure[None, :], 1 << 14, tickets)
    merit = tickets * amount + jnp.arange(amount)
    return lax.top_k(merit.astype(jnp.int32), top)[1].astype(jnp.int32)


def gaussian(own_key, shape, width, most, cuts=(), kind=jnp.bfloat16):
    array = width * jax.random.normal(own_key, shape, jnp.float32)
    if cuts:
        array = array * shard_levels(own_key, shape, cuts, -0.22, 0.18)
    return jnp.clip(array, -most, most).astype(kind)


def setup_inputs(seed: int = 0) -> dict:
    arg_keys = jax.random.split(jax.random.key(seed), 13)
    return {
        "tokens": gaussian(arg_keys[0], (TOKENS, D), 1.0, 6.0, ((0, 16),)),
        "cotangent": gaussian(arg_keys[1], (TOKENS, D), 1.0, 6.0, ((0, 16),)),
        "norm_gains": jnp.clip(1.0 + 0.1 * jax.random.normal(arg_keys[2], (2, 2, D), jnp.float32), 0.5, 1.5),
        "norm_biases": gaussian(arg_keys[3], (2, 2, D), 0.3, 1.5, ((0, 2),), jnp.float32),
        "qkv_weight": draw_qkv_weight(jax.random.fold_in(arg_keys[12], 71), 0),
        "out_weight": gaussian(arg_keys[5], (2, D, D), (max(2, 4 * D // SEQ)) ** -0.5, 1.5, ((0, 2),)),
        "dense_in": gaussian(arg_keys[6], (D, FF), D ** -0.5, 0.21875),
        "dense_out": gaussian(arg_keys[7], (FF, D), FF ** -0.5, 0.109375),
        "expert_in": gaussian(arg_keys[8], (EXPERTS, D, FF), D ** -0.5, 0.21875, ((0, 4), (2, 4))),
        "expert_out": gaussian(arg_keys[9], (EXPERTS, FF, D), FF ** -0.5, 0.109375, ((0, 4), (1, 4))),
        "routes": distinct(arg_keys[10], TOKENS, EXPERTS, 2, 8192),
        "gates": jnp.clip(0.1 + 0.5 * jax.random.uniform(arg_keys[11], (TOKENS, 2), jnp.float32) ** shard_levels(arg_keys[11], (TOKENS, 2), ((0, 16),), -0.2, 0.2), 0.1, 0.6),
    }


eps = 1e-06

def layer_norm(values, gain, bias):
    centred = values - lax.optimization_barrier(jnp.mean(values, axis=-1, keepdims=True))
    spread = lax.optimization_barrier(jnp.mean(centred * centred, axis=-1, keepdims=True))
    return centred * lax.rsqrt(spread + eps) * gain + bias

def norm_back(values, gain, bias, cotan):
    _, pull = jax.vjp(layer_norm, values, gain, bias)
    return pull(cotan)

def gelu_back(before, cotan):
    _, pull = jax.vjp(jax.nn.gelu, before)
    return pull(cotan)[0]

def matmul(left, right):
    return jnp.dot(left, right, preferred_element_type=jnp.float32)

def matmul_rows(left, right):
    return jnp.dot(left.T, right, preferred_element_type=jnp.float32)

def matmul_cols(left, right):
    return jnp.dot(left, right.T, preferred_element_type=jnp.float32)

def widen(values):
    return lax.optimization_barrier(values).astype(jnp.float32)

def head_split(mixed):
    return widen(mixed).reshape(-1, SEQ, 3, HEADS, HEAD_DIM)

def score_table(split):
    return jnp.einsum('bqhd,bkhd->bhqk', split[:, :, 0], split[:, :, 1]) * HEAD_DIM ** (-0.5)

def attend(normed, weight_qkv):
    mixed = matmul(normed, weight_qkv).astype(jnp.bfloat16)
    split = head_split(mixed)
    scores = score_table(split)
    top = lax.optimization_barrier(jnp.max(scores, axis=-1, keepdims=True))
    logsum = top + jnp.log(lax.optimization_barrier(jnp.sum(jnp.exp(scores - top), axis=-1, keepdims=True)))
    probs = widen(jnp.exp(scores - logsum).astype(jnp.bfloat16))
    attended = jnp.einsum('bhqk,bkhd->bqhd', probs, split[:, :, 2])
    return (mixed, logsum, attended.reshape(normed.shape[0], D).astype(jnp.bfloat16))

def attend_back(normed, mixed, logsum, attended, grad_hidden, weight_qkv, weight_out):
    grad_cast = grad_hidden.astype(jnp.bfloat16)
    grad_wout = matmul_rows(attended, grad_cast)
    grad_att = matmul_cols(grad_cast, weight_out).astype(jnp.bfloat16)
    split = head_split(mixed)
    probs_full = jnp.exp(score_table(split) - logsum)
    probs = widen(probs_full.astype(jnp.bfloat16))
    grad_heads = widen(grad_att).reshape(-1, SEQ, HEADS, HEAD_DIM)
    grad_probs = jnp.einsum('bqhd,bkhd->bhqk', grad_heads, split[:, :, 2])
    grad_value = jnp.einsum('bhqk,bqhd->bkhd', probs, grad_heads)
    inner = lax.optimization_barrier(jnp.sum(probs_full * grad_probs, axis=-1, keepdims=True))
    grad_scores = widen((probs_full * (grad_probs - inner) * HEAD_DIM ** (-0.5)).astype(jnp.bfloat16))
    grad_query = jnp.einsum('bhqk,bkhd->bqhd', grad_scores, split[:, :, 1])
    grad_key = jnp.einsum('bhqk,bqhd->bkhd', grad_scores, split[:, :, 0])
    grad_mixed = jnp.stack([grad_query, grad_key, grad_value], axis=2).reshape(normed.shape[0], 3 * D).astype(jnp.bfloat16)
    return (matmul_cols(grad_mixed, weight_qkv), matmul_rows(normed, grad_mixed), grad_wout)

def front_half(block_in, gains, biases, weight_qkv, weight_out):
    start = block_in.astype(jnp.float32)
    normed = layer_norm(start, gains[0], biases[0]).astype(jnp.bfloat16)
    mixed, logsum, attended = attend(normed, weight_qkv)
    hidden = start + matmul(attended, weight_out)
    second = layer_norm(hidden, gains[1], biases[1]).astype(jnp.bfloat16)
    return (normed, mixed, logsum, attended, hidden, second)

def front_back(block_in, saved, grad_top, grad_second, gains, biases, weight_qkv, weight_out):
    normed, mixed, logsum, attended, hidden = saved
    grad_mid, gain_two, bias_two = norm_back(hidden, gains[1], biases[1], grad_second)
    grad_hidden = grad_top + grad_mid
    grad_normed, grad_wqkv, grad_wout = attend_back(normed, mixed, logsum, attended, grad_hidden, weight_qkv, weight_out)
    grad_start, gain_one, bias_one = norm_back(block_in.astype(jnp.float32), gains[0], biases[0], grad_normed)
    return (grad_start + grad_hidden, grad_wqkv, grad_wout, jnp.stack([gain_one, gain_two]), jnp.stack([bias_one, bias_two]))

def route(chosen):
    flat = jnp.concatenate([chosen[:, 0], chosen[:, 1]]).astype(jnp.int32)
    table = (flat[:, None] == jnp.arange(EXPERTS, dtype=jnp.int32)[None, :]).astype(jnp.int32)
    place = lax.optimization_barrier(jnp.sum((jnp.cumsum(table, axis=0, dtype=jnp.int32) - table) * table, axis=1, dtype=jnp.int32))
    kept = place < CAP
    slot = jnp.where(kept, flat * CAP + place, EXPERTS * CAP).astype(jnp.int32)
    return (slot, kept)

def place_rows(values, slot):
    return jnp.zeros((EXPERTS * CAP, D), jnp.bfloat16).at[slot].set(values, mode='drop')

def pick_rows(buffer, slot, kept, factor):
    picked = jnp.take(buffer, jnp.where(kept, slot, 0).astype(jnp.int32), axis=0).astype(jnp.float32) * factor[:, None]
    return picked[:ROWS] + picked[ROWS:]

def expert_pass(inputs):
    rows_in, grad_rows, weight_in, weight_back = inputs
    before = matmul(rows_in, weight_in)
    active = jax.nn.gelu(before).astype(jnp.bfloat16)
    returned = matmul(active, weight_back).astype(jnp.bfloat16)
    grad_active = matmul_cols(grad_rows, weight_back)
    grad_back = matmul_rows(active, grad_rows)
    grad_before = gelu_back(before, grad_active).astype(jnp.bfloat16)
    grad_in = matmul_rows(rows_in, grad_before)
    grad_input = matmul_cols(grad_before, weight_in).astype(jnp.bfloat16)
    return (returned, grad_input, grad_in, grad_back)

def reference(tokens, cotangent, norm_gains, norm_biases, qkv_weight, out_weight, dense_in, dense_out, expert_in, expert_out, routes, gates):
    blocks = TOKENS // ROWS
    gain_all = norm_gains.astype(jnp.float32)
    bias_all = norm_biases.astype(jnp.float32)
    token_blocks = tokens.reshape(blocks, ROWS, D)
    grad_blocks = cotangent.reshape(blocks, ROWS, D)
    route_blocks = routes.reshape(blocks, ROWS, 2)
    gate_blocks = gates.reshape(blocks, ROWS, 2)

    def first_forward(block_in):
        outs = front_half(block_in, gain_all[0], bias_all[0], qkv_weight[0], out_weight[0])
        active = jax.nn.gelu(matmul(outs[5], dense_in)).astype(jnp.bfloat16)
        return (outs[4] + matmul(active, dense_out)).astype(jnp.bfloat16)
    middle = lax.map(first_forward, token_blocks)

    def second_front(inputs):
        block_in, chosen, gate_pair, grad_block = inputs
        second = front_half(block_in, gain_all[1], bias_all[1], qkv_weight[1], out_weight[1])[5]
        slot, kept = route(chosen)
        gate_flat = jnp.concatenate([gate_pair[:, 0], gate_pair[:, 1]])
        grad_top = grad_block.astype(jnp.float32)
        grad_sent = (jnp.concatenate([grad_top, grad_top]) * gate_flat[:, None]).astype(jnp.bfloat16)
        return (place_rows(jnp.concatenate([second, second]), slot), place_rows(grad_sent, slot))
    outgoing, grad_outgoing = lax.map(second_front, (middle, route_blocks, gate_blocks, grad_blocks))

    def by_expert(values):
        return jnp.swapaxes(values.reshape(blocks, EXPERTS, CAP, D), 0, 1).reshape(EXPERTS, blocks * CAP, D)

    def by_block(values):
        return jnp.swapaxes(values.reshape(EXPERTS, blocks, CAP, D), 0, 1).reshape(blocks, EXPERTS * CAP, D)
    returned, grad_returned, expert_in_grad, expert_out_grad = lax.map(expert_pass, (by_expert(outgoing), by_expert(grad_outgoing), expert_in, expert_out))

    def second_back(carry, inputs):
        block_in, chosen, gate_pair, grad_block, back_home, grad_home = inputs
        normed, mixed, logsum, attended, hidden, second = front_half(block_in, gain_all[1], bias_all[1], qkv_weight[1], out_weight[1])
        slot, kept = route(chosen)
        gate_flat = jnp.concatenate([gate_pair[:, 0], gate_pair[:, 1]])
        final = hidden + pick_rows(back_home, slot, kept, jnp.where(kept, gate_flat, 0.0))
        grad_second = pick_rows(grad_home, slot, kept, kept.astype(jnp.float32))
        grad_start, grad_wqkv, grad_wout, grad_gain, grad_bias = front_back(block_in, (normed, mixed, logsum, attended, hidden), grad_block.astype(jnp.float32), grad_second, gain_all[1], bias_all[1], qkv_weight[1], out_weight[1])
        carry = (carry[0] + grad_wqkv, carry[1] + grad_wout, carry[2] + grad_gain, carry[3] + grad_bias)
        return (carry, (final.astype(jnp.bfloat16), grad_start))
    shared_zero = (jnp.zeros((D, 3 * D), jnp.float32), jnp.zeros((D, D), jnp.float32), jnp.zeros((2, D), jnp.float32), jnp.zeros((2, D), jnp.float32))
    second_sums, (final, grad_middle) = lax.scan(second_back, shared_zero, (middle, route_blocks, gate_blocks, grad_blocks, by_block(returned), by_block(grad_returned)))

    def first_back(carry, inputs):
        block_in, grad_block = inputs
        normed, mixed, logsum, attended, hidden, second = front_half(block_in, gain_all[0], bias_all[0], qkv_weight[0], out_weight[0])
        before = matmul(second, dense_in)
        active = jax.nn.gelu(before).astype(jnp.bfloat16)
        grad_result = grad_block.astype(jnp.bfloat16)
        grad_back = matmul_rows(active, grad_result)
        grad_before = gelu_back(before, matmul_cols(grad_result, dense_out)).astype(jnp.bfloat16)
        grad_in = matmul_rows(second, grad_before)
        grad_second = matmul_cols(grad_before, dense_in)
        grad_start, grad_wqkv, grad_wout, grad_gain, grad_bias = front_back(block_in, (normed, mixed, logsum, attended, hidden), widen(grad_result), grad_second, gain_all[0], bias_all[0], qkv_weight[0], out_weight[0])
        carry = (carry[0] + grad_wqkv, carry[1] + grad_wout, carry[2] + grad_gain, carry[3] + grad_bias, carry[4] + grad_in, carry[5] + grad_back)
        return (carry, grad_start)
    first_zero = shared_zero + (jnp.zeros((D, FF), jnp.float32), jnp.zeros((FF, D), jnp.float32))
    first_sums, grad_tokens = lax.scan(first_back, first_zero, (token_blocks, grad_middle))
    acts = jnp.stack([middle.reshape(TOKENS, D), final.reshape(TOKENS, D)])
    act_grads = jnp.stack([grad_tokens.reshape(TOKENS, D), grad_middle.reshape(TOKENS, D)])
    qkv_grad = jnp.stack([first_sums[0], second_sums[0]])
    out_grad = jnp.stack([first_sums[1], second_sums[1]])
    gain_grad = jnp.stack([first_sums[2], second_sums[2]])
    bias_grad = jnp.stack([first_sums[3], second_sums[3]])
    return (acts, act_grads, qkv_grad, out_grad, gain_grad, bias_grad, first_sums[4], first_sums[5], expert_in_grad, expert_out_grad)
```

```python
import jax
import jax.numpy as jnp
from jax import lax
from jax.sharding import PartitionSpec as P

HEADS = 12
HEAD_DIM = 64
SEQ = 197


eps = 1e-06


def pair(block):
    return lax.ppermute(block, "section", [(0, 1), (1, 0)])


def layer_norm(values, gain, bias):
    centred = values - jnp.mean(values, axis=-1, keepdims=True)
    spread = jnp.mean(centred * centred, axis=-1, keepdims=True)
    return centred * lax.rsqrt(spread + eps) * gain + bias


def norm_back(values, gain, bias, cotan):
    _, pull = jax.vjp(layer_norm, values, gain, bias)
    return pull(cotan)


def gelu_back(before, cotan):
    _, pull = jax.vjp(jax.nn.gelu, before)
    return pull(cotan)[0]


def matmul(left, right):
    return jnp.dot(left, right, preferred_element_type=jnp.float32)


def matmul_rows(left, right):
    return lax.dot_general(
        left, right, (((0,), (0,)), ((), ())), preferred_element_type=jnp.float32
    )


def matmul_cols(left, right):
    return lax.dot_general(
        left, right, (((1,), (1,)), ((), ())), preferred_element_type=jnp.float32
    )


def head_split(mixed):
    return mixed.reshape(-1, SEQ, 3, HEADS, HEAD_DIM)


def score_table(split):
    return jnp.einsum(
        "bqhd,bkhd->bhqk", split[:, :, 0], split[:, :, 1], preferred_element_type=jnp.float32
    ) * HEAD_DIM ** (-0.5)


def attend(normed, weight_qkv):
    mixed = matmul(normed, weight_qkv).astype(jnp.bfloat16)
    split = head_split(mixed)
    scores = score_table(split)
    top = jnp.max(scores, axis=-1, keepdims=True)
    logsum = top + jnp.log(jnp.sum(jnp.exp(scores - top), axis=-1, keepdims=True))
    probs = jnp.exp(scores - logsum).astype(jnp.bfloat16)
    attended = jnp.einsum(
        "bhqk,bkhd->bqhd", probs, split[:, :, 2], preferred_element_type=jnp.float32
    )
    return (mixed, logsum, attended.reshape(normed.shape[0], -1).astype(jnp.bfloat16))


def attend_back(normed, mixed, logsum, attended, grad_hidden, weight_qkv, weight_out):
    grad_cast = grad_hidden.astype(jnp.bfloat16)
    grad_wout = matmul_rows(attended, grad_cast).astype(jnp.bfloat16)
    grad_att = matmul_cols(grad_cast, weight_out).astype(jnp.bfloat16)
    split = head_split(mixed)
    probs_full = jnp.exp(score_table(split) - logsum)
    probs = probs_full.astype(jnp.bfloat16)
    grad_heads = grad_att.reshape(-1, SEQ, HEADS, HEAD_DIM)
    grad_probs = jnp.einsum(
        "bqhd,bkhd->bhqk", grad_heads, split[:, :, 2], preferred_element_type=jnp.float32
    )
    grad_value = jnp.einsum(
        "bhqk,bqhd->bkhd", probs, grad_heads, preferred_element_type=jnp.float32
    )
    inner = jnp.sum(probs_full * grad_probs, axis=-1, keepdims=True)
    grad_scores = (probs_full * (grad_probs - inner) * HEAD_DIM ** (-0.5)).astype(jnp.bfloat16)
    grad_query = jnp.einsum(
        "bhqk,bkhd->bqhd", grad_scores, split[:, :, 1], preferred_element_type=jnp.float32
    )
    grad_key = jnp.einsum(
        "bhqk,bqhd->bkhd", grad_scores, split[:, :, 0], preferred_element_type=jnp.float32
    )
    grad_mixed = (
        jnp.stack([grad_query, grad_key, grad_value], axis=2)
        .reshape(normed.shape[0], -1)
        .astype(jnp.bfloat16)
    )
    return (
        matmul_cols(grad_mixed, weight_qkv),
        matmul_rows(normed, grad_mixed).astype(jnp.bfloat16),
        grad_wout,
    )


def front_half(block_in, gains, biases, weight_qkv, weight_out):
    start = block_in.astype(jnp.float32)
    normed = layer_norm(start, gains[0], biases[0]).astype(jnp.bfloat16)
    mixed, logsum, attended = attend(normed, weight_qkv)
    hidden = start + matmul(attended, weight_out)
    second = layer_norm(hidden, gains[1], biases[1]).astype(jnp.bfloat16)
    return (normed, mixed, logsum, attended, hidden, second)


def front_back(block_in, saved, grad_top, grad_second, gains, biases, weight_qkv, weight_out):
    normed, mixed, logsum, attended, hidden = saved
    grad_mid, gain_two, bias_two = norm_back(hidden, gains[1], biases[1], grad_second)
    grad_hidden = grad_top + grad_mid
    grad_normed, grad_wqkv, grad_wout = attend_back(
        normed, mixed, logsum, attended, grad_hidden, weight_qkv, weight_out
    )
    grad_start, gain_one, bias_one = norm_back(
        block_in.astype(jnp.float32), gains[0], biases[0], grad_normed
    )
    return (
        grad_start + grad_hidden,
        grad_wqkv,
        grad_wout,
        jnp.stack([gain_one, gain_two, bias_one, bias_two], axis=1),
    )


def rounded(values):
    return lax.reduce_precision(values, exponent_bits=8, mantissa_bits=7).astype(jnp.bfloat16)


def on_device(
    tokens,
    cotangent,
    norm_gains,
    norm_biases,
    qkv_weight,
    out_weight,
    dense_in,
    dense_out,
    expert_in,
    expert_out,
    routes,
    gates,
):
    rows = SEQ
    width = tokens.shape[1]
    experts = lax.axis_size("experts")
    capacity = 2 * rows // experts
    slots = experts * capacity
    section = lax.axis_index("section")
    first = section == 0
    everyone = ("experts", "dp")

    def ordered(mine, other, axis):
        return jnp.concatenate(
            [jnp.where(first, mine, other), jnp.where(first, other, mine)], axis=axis
        )

    def kept_half(array, axis):
        low, high = jnp.split(array, 2, axis=axis)
        return jnp.where(first, low, high)

    def sent_half(array, axis):
        low, high = jnp.split(array, 2, axis=axis)
        return jnp.where(first, high, low)

    def pair_sum(array):
        landed = pair(sent_half(array, 1)).astype(jnp.float32)
        return (kept_half(array, 1).astype(jnp.float32) + landed).astype(jnp.bfloat16)

    def scattered(array, axes):
        return lax.psum_scatter(array, axes, scatter_dimension=0, tiled=True)

    def both(own):
        other = pair(own)
        return (jnp.where(first, own, other), jnp.where(first, other, own))

    qkv_zero, qkv_one = both(qkv_weight[0])
    norms_zero, norms_one = both(jnp.concatenate([norm_gains[0], norm_biases[0]], axis=0))
    out_zero, out_one = both(out_weight[0])
    part_in = lax.all_gather(kept_half(expert_in[0], 0), "dp", axis=1, tiled=True)
    part_back = lax.all_gather(kept_half(expert_out[0], 1), "dp", axis=0, tiled=True)
    weight_in = ordered(part_in, pair(part_in), 0)
    weight_back = ordered(part_back, pair(part_back), 1)

    def own_block(array):
        return lax.dynamic_slice_in_dim(array, section * rows, rows, 0)

    block_in = own_block(tokens)
    grad_top = own_block(cotangent).astype(jnp.float32)
    chosen = own_block(routes)
    gate_pair = own_block(gates)

    flat = jnp.concatenate([chosen[:, 0], chosen[:, 1]])
    table = (flat[:, None] == jnp.arange(experts, dtype=jnp.int32)[None, :]).astype(jnp.int32)
    place = jnp.sum(
        (jnp.cumsum(table, axis=0, dtype=jnp.int32) - table) * table, axis=1, dtype=jnp.int32
    )
    slot = jnp.where(place < capacity, flat * capacity + place, slots)
    gate_flat = jnp.concatenate([gate_pair[:, 0], gate_pair[:, 1]])
    spread = (jnp.arange(slots, dtype=jnp.int32)[:, None] == slot[None, :]).astype(jnp.bfloat16)

    normed0, mixed0, logsum0, attended0, hidden0, second0 = front_half(
        block_in, norms_zero[:2], norms_zero[2:], qkv_zero, out_zero
    )
    before0 = matmul(second0, dense_in)
    active0 = jax.nn.gelu(before0).astype(jnp.bfloat16)
    middle = rounded(hidden0 + matmul(active0, dense_out))

    normed1, mixed1, logsum1, attended1, hidden1, second1 = front_half(
        middle, norms_one[:2], norms_one[2:], qkv_one, out_one
    )
    doubled = jnp.concatenate([grad_top, grad_top]) * gate_flat[:, None]
    outgoing = jnp.concatenate(
        [
            matmul(spread[:, :rows] + spread[:, rows:], second1).astype(jnp.bfloat16),
            matmul(spread, doubled.astype(jnp.bfloat16)).astype(jnp.bfloat16),
        ],
        axis=1,
    )
    arrived = lax.all_to_all(
        outgoing.reshape(experts, capacity, 2 * width),
        "experts",
        split_axis=0,
        concat_axis=0,
        tiled=True,
    ).reshape(slots, 2 * width)
    rows_in = arrived[:, :width]
    grad_rows = arrived[:, width:]
    before1 = matmul(rows_in, weight_in)
    active1 = jax.nn.gelu(before1).astype(jnp.bfloat16)
    returned = matmul(active1, weight_back).astype(jnp.bfloat16)
    grad_before1 = gelu_back(before1, matmul_cols(grad_rows, weight_back)).astype(jnp.bfloat16)
    grad_arrived = matmul_cols(grad_before1, weight_in).astype(jnp.bfloat16)
    home = lax.all_to_all(
        jnp.concatenate([returned, grad_arrived], axis=1).reshape(experts, capacity, 2 * width),
        "experts",
        split_axis=0,
        concat_axis=0,
        tiled=True,
    ).reshape(slots, 2 * width)
    expert_in_sum = scattered(
        pair_sum(matmul_rows(grad_before1, rows_in).astype(jnp.bfloat16)), "dp"
    )
    expert_out_sum = scattered(
        pair_sum(matmul_rows(active1, grad_rows).astype(jnp.bfloat16)), "dp"
    )

    picked = matmul_rows(spread, home[:, :width]) * gate_flat[:, None]
    final = (hidden1 + (picked[:rows] + picked[rows:])).astype(jnp.bfloat16)
    grad_second1 = matmul_rows(spread[:, :rows] + spread[:, rows:], home[:, width:])
    grad_middle, grad_qkv1, grad_out1, grad_norm1 = front_back(
        middle,
        (normed1, mixed1, logsum1, attended1, hidden1),
        grad_top,
        grad_second1,
        norms_one[:2],
        norms_one[2:],
        qkv_one,
        out_one,
    )
    shared1 = scattered(
        jnp.concatenate([pair_sum(grad_qkv1), pair_sum(grad_out1)], axis=1), everyone
    )

    grad_result = rounded(grad_middle)
    dense_out_sum = scattered(
        pair_sum(matmul_rows(active0, grad_result).astype(jnp.bfloat16)), everyone
    )
    grad_before0 = gelu_back(before0, matmul_cols(grad_result, dense_out)).astype(jnp.bfloat16)
    dense_in_sum = scattered(
        pair_sum(matmul_rows(second0, grad_before0).astype(jnp.bfloat16)), everyone
    )
    grad_tokens, grad_qkv0, grad_out0, grad_norm0 = front_back(
        block_in,
        (normed0, mixed0, logsum0, attended0, hidden0),
        grad_result.astype(jnp.float32),
        matmul_cols(grad_before0, dense_in),
        norms_zero[:2],
        norms_zero[2:],
        qkv_zero,
        out_zero,
    )
    shared0 = scattered(
        jnp.concatenate([pair_sum(grad_qkv0), pair_sum(grad_out0)], axis=1), everyone
    )
    norm_sum = scattered(
        jnp.where(first, grad_norm0, grad_norm1)
        + pair(jnp.where(first, grad_norm1, grad_norm0)),
        everyone,
    )

    own_shared = jnp.where(first, shared0, shared1)
    other_shared = pair(jnp.where(first, shared1, shared0))
    cut = qkv_weight.shape[2] // 2
    qkv_sum = ordered(own_shared[:, :cut], other_shared[:, :cut], 1).astype(jnp.float32)
    out_sum = ordered(own_shared[:, cut:], other_shared[:, cut:], 1).astype(jnp.float32)
    acts = ordered(
        jnp.where(first, middle, final), pair(jnp.where(first, final, middle)), 0
    )
    act_grads = ordered(
        jnp.where(first, grad_tokens, grad_middle),
        pair(jnp.where(first, grad_middle, grad_tokens)),
        0,
    )
    return (
        acts[None],
        act_grads[None],
        qkv_sum[None],
        out_sum[None],
        norm_sum[:, :2].T[None],
        norm_sum[:, 2:].T[None],
        dense_in_sum.astype(jnp.float32),
        dense_out_sum.astype(jnp.float32),
        expert_in_sum.astype(jnp.float32).T[None],
        expert_out_sum.astype(jnp.float32)[None],
    )


def solution(mesh):
    placed = (
        P(("experts", "dp"), None),
        P(("experts", "dp"), None),
        P("section", None, None),
        P("section", None, None),
        P("section", None, None),
        P("section", None, None),
        P(),
        P(),
        P("experts", None, "dp"),
        P("experts", "dp", None),
        P(("experts", "dp"), None),
        P(("experts", "dp"), None),
    )
    return jax.shard_map(
        on_device,
        mesh=mesh,
        in_specs=placed,
        out_specs=(
            P("section", ("experts", "dp"), None),
            P("section", ("experts", "dp"), None),
            P("section", ("experts", "dp"), None),
            P("section", ("experts", "dp"), None),
            P("section", None, ("experts", "dp")),
            P("section", None, ("experts", "dp")),
            P(("experts", "dp"), "section"),
            P(("experts", "dp"), "section"),
            P("experts", "section", "dp"),
            P("experts", "dp", "section"),
        ),
        check_vma=False,
    )
```
